256 devices in a mesh: band: 32 (over z_hi, y, x), strip: 8 (over z_lo, core).
Axes of the slice: x: 4, y: 4, z: 8 (z_hi: 2, z_lo: 4; z = z_hi * 4 + z_lo), core: 2. Of those that a mesh axis runs over, the one named last changes fastest.
Arguments:
- coeffs: bfloat16 [512, 128, 4096], P('strip', None, 'band'), may hold values from -4.1875 to 4.1875
- hamiltonian: bfloat16 [512, 5, 128, 128], P('strip'), may hold values from -0.15625 to 0.15625
- adjacency: int32 [512, 5], P('strip'), may hold values from 0 to 511, as said below
- occupation: float32 [4096], P('band'), may hold values from 0.1 to 2
Outputs:
- density: float32 [512, 128, 128], P(('strip', 'band'))
The draws below stay inside these ranges and needn't reach their ends.
Inputs may be any that keep to these rules, and one draw needn't show every extreme that they name: `adjacency`: row e lists element e itself and its four neighbours on the periodic 32 x 16 sheet of elements, numbered row * 16 + column, in an order drawn for each element.
All inputs are finite; a program needn't handle non-finite values.
Results may differ from the reference program's by a relative error of at most 0.019.
Values may be sent and summed in bfloat16 or wider, within the bound.
No kernel may reach another device: no remote copies, remote signals or barrier semaphores. Data moves between devices by JAX's collectives and lax.ppermute only.
A program may use at most 128 MiB of HBM per device.

```python
import math
import jax
import jax.numpy as jnp
from jax import lax

NB = 128
EY = 16
EX = 32
ELEMS = 512
NBAND = 4096


def draw_adjacency(key, part):
    element = jnp.arange(ELEMS, dtype=jnp.int32)
    elem_row = element // EY
    elem_col = element % EY
    candidates = jnp.stack([element, (elem_row + 1) % EX * EY + elem_col, (elem_row - 1 + EX) % EX * EY + elem_col, elem_row * EY + (elem_col + 1) % EY, elem_row * EY + (elem_col - 1 + EY) % EY], axis=1)
    scores = jax.random.randint(key, (ELEMS, 5), 0, 1 << 20, dtype=jnp.int32) * 8 + jnp.arange(5, dtype=jnp.int32)
    ordering = jnp.argsort(scores, axis=1, stable=True)
    return jnp.take_along_axis(candidates, ordering, axis=1).astype(jnp.int32)


def shard_levels(own_key, extent, cuts, least, top_value):
    def one(axis_at, parts):
        heights = jax.random.uniform(jax.random.fold_in(jax.random.fold_in(own_key, 6), axis_at), (parts,), jnp.float32, least / len(cuts), top_value / len(cuts))
        return jnp.repeat(jnp.exp(heights), extent[axis_at] // parts).reshape((-1,) + (1,) * (len(extent) - axis_at - 1))

    factor_of = one(*cuts[0])
    for cut in cuts[1:]:
        factor_of = factor_of * one(*cut)
    return factor_of


def scatter_about(stream_key, shape, scale, most, shards=(), held_as=jnp.bfloat16):
    values = scale * jax.random.normal(stream_key, shape, jnp.float32)
    if shards:
        values = values * shard_levels(stream_key, shape, shards, -0.22, 0.18)
    return jnp.clip(values, -most, most).astype(held_as)


def setup_inputs(seed: int = 0) -> dict:
    splits = jax.random.split(jax.random.key(seed), 5)
    return {
        "coeffs": scatter_about(splits[0], (ELEMS, NB, NBAND), 0.7, 4.1875, ((0, 8), (2, 32))),
        "hamiltonian": scatter_about(splits[1], (ELEMS, 5, NB, NB), (10 * NB) ** -0.5, 0.15625, ((0, 8),)),
        "adjacency": draw_adjacency(jax.random.fold_in(splits[4], 71), 0),
        "occupation": jnp.clip(jnp.exp(math.log(2.0) - 2.9957323 * jax.random.uniform(splits[3], (NBAND,), jnp.float32) ** shard_levels(splits[3], (NBAND,), ((0, 32),), -0.2, 0.2)), 0.1, 2.0),
    }


def apply_operator(field_block, hamiltonian_wide, adjacency):
    total = jnp.zeros(field_block.shape, jnp.float32)
    for slot_index in range(5):
        neighbours = field_block[adjacency[:, slot_index]].astype(jnp.float32)
        total = total + jnp.einsum("eik,ekb->eib", hamiltonian_wide[:, slot_index], neighbours)
    return total


def reference(coeffs, hamiltonian, adjacency, occupation):
    hamiltonian_wide = hamiltonian.astype(jnp.float32)
    block_width = math.gcd(NBAND, 512)
    blocks = NBAND // block_width
    coeff_blocks = jnp.moveaxis(coeffs.reshape(ELEMS, NB, blocks, block_width), 2, 0)
    occ_blocks = occupation.reshape(blocks, block_width)

    def one_block(accumulated, inputs):
        coeff_block, occ_block = inputs
        degree_one = apply_operator(coeff_block, hamiltonian_wide, adjacency).astype(jnp.bfloat16)
        degree_two = (2.0 * apply_operator(degree_one, hamiltonian_wide, adjacency) - coeff_block.astype(jnp.float32)).astype(jnp.bfloat16)
        filtered = (2.0 * apply_operator(degree_two, hamiltonian_wide, adjacency) - degree_one.astype(jnp.float32)).astype(jnp.bfloat16)
        weighted = (filtered.astype(jnp.float32) * occ_block).astype(jnp.bfloat16)
        accumulated = accumulated + jnp.einsum("eib,ejb->eij", weighted.astype(jnp.float32), filtered.astype(jnp.float32))
        return accumulated, None

    summed, unused = lax.scan(one_block, jnp.zeros((ELEMS, NB, NB), jnp.float32), (coeff_blocks, occ_blocks))
    return summed / NBAND
```

```python
import functools

import jax
import jax.numpy as jnp
from jax import lax
from jax.experimental import pallas as pl
from jax.experimental.pallas import tpu as pltpu
from jax.sharding import PartitionSpec as P

EY = 16
EXS = 4
EX = 32
NB = 128
NBAND = 4096
XS = 4
YS = 4

BF = jnp.bfloat16
F32 = jnp.float32
VMEM = pltpu.VMEM


def struct(shape, dtype):
    return jax.ShapeDtypeStruct(shape, dtype)


def vmem_specs(count):
    return [pl.BlockSpec(memory_space=VMEM)] * count


def dot(a, b):
    return jnp.dot(a, b, preferred_element_type=F32)


def gram(a, b):
    return lax.dot_general(a, b, (((1,), (1,)), ((), ())), preferred_element_type=F32)


def block_indices(adjacency, strip_index):
    local = jnp.arange(EXS * EY, dtype=jnp.int32)
    row = strip_index * EXS + local // EY
    col = local % EY
    wanted = jnp.stack(
        [
            row * EY + col,
            (row + 1) % EX * EY + col,
            (row + EX - 1) % EX * EY + col,
            row * EY + (col + 1) % EY,
            row * EY + (col + EY - 1) % EY,
        ],
        axis=1,
    )
    hit = adjacency[:, None, :] == wanted[:, :, None]
    slot = jnp.sum(jnp.where(hit, jnp.arange(5, dtype=jnp.int32), 0), axis=2)
    return (local[:, None] * 5 + slot).reshape(-1)


def sweep_kernel(level, index_ref, *refs):
    if level == 1:
        v_ref, h_ref, mid_ref, part0, part3, far0, far3, h, sem = refs
        rows = [v_ref.at[pl.ds(r * EY, EY)] for r in range(EXS)]
        before = None
    else:
        v0, vm, v3, p0, pm, p3, h_ref, mid_ref, part0, part3, h, sem = refs
        rows = [v0, vm.at[pl.ds(0, EY)], vm.at[pl.ds(EY, EY)], v3]
        before = [p0, pm.at[pl.ds(0, EY)], pm.at[pl.ds(EY, EY)], p3]
    per_row = 5 * EY
    copies = [
        pltpu.make_async_copy(
            h_ref.at[pl.ds(r * per_row, per_row)], h.at[pl.ds(r * per_row, per_row)], sem.at[r]
        )
        for r in range(EXS)
    ]
    for copy in copies:
        copy.start()
    for r in range(EXS):
        copies[r].wait()

        def element(c, carry, r=r):
            at = (r * EY + c) * 5
            right = lax.rem(c + 1, EY)
            left = lax.rem(c + EY - 1, EY)
            terms = [(0, rows[r][c]), (3, rows[r][right]), (4, rows[r][left])]
            if r + 1 < EXS:
                terms.append((1, rows[r + 1][c]))
            if r > 0:
                terms.append((2, rows[r - 1][c]))
            a = jnp.concatenate([h[index_ref[at + k]] for k, _ in terms], axis=1)
            b = jnp.concatenate([v for _, v in terms], axis=0)
            total = dot(a, b)
            if before is not None:
                total = 2.0 * total - before[r][c].astype(F32)
            if r == 0:
                part0[c] = total
                if level == 1:
                    far0[c] = h[index_ref[at + 2]]
            elif r == EXS - 1:
                part3[c] = total
                if level == 1:
                    far3[c] = h[index_ref[at + 1]]
            else:
                mid_ref[(r - 1) * EY + c] = total.astype(BF)
            return carry

        lax.fori_loop(0, EY, element, 0, unroll=2)


def sweep(level, index, fields, blocks):
    row = (EY, NB, NB)
    outs = [struct((2 * EY, NB, NB), BF), struct(row, F32), struct(row, F32)]
    if level == 1:
        outs += [struct(row, BF), struct(row, BF)]
    count = 64 * 5
    return pl.pallas_call(
        functools.partial(sweep_kernel, level),
        out_shape=outs,
        in_specs=[pl.BlockSpec(memory_space=pltpu.SMEM)]
        + vmem_specs(len(fields))
        + [pl.BlockSpec(memory_space=pl.ANY)],
        out_specs=vmem_specs(len(outs)),
        scratch_shapes=[VMEM((count, NB, NB), BF), pltpu.SemaphoreType.DMA((EXS,))],
        compiler_params=pltpu.CompilerParams(vmem_limit_bytes=40 << 20),
        name=f"sweep{level}",
    )(index, *fields, blocks)


def edge_kernel(scale, part_ref, far_ref, halo_ref, out_ref):
    def element(c, carry):
        out_ref[c] = (part_ref[c] + scale * dot(far_ref[c], halo_ref[c])).astype(BF)
        return carry

    lax.fori_loop(0, EY, element, 0, unroll=4)


def edge(level, part, far, halo):
    return pl.pallas_call(
        functools.partial(edge_kernel, 1.0 if level == 1 else 2.0),
        out_shape=struct((EY, NB, NB), BF),
        in_specs=vmem_specs(3),
        out_specs=pl.BlockSpec(memory_space=VMEM),
        compiler_params=pltpu.CompilerParams(vmem_limit_bytes=16 << 20),
        name=f"edge{level}",
    )(part, far, halo)


def element_of(x, k):
    return (k // 2) * 8 + 2 * x + k % 2


def scaled_kernel(rows, me_ref, root_ref, *refs):
    srcs, outs = refs[: len(rows)], refs[len(rows) :]
    root = root_ref[...]
    for s in range(XS):
        x = lax.rem(me_ref[0] + s, XS)
        for n, offset in enumerate(rows):
            for k in range(4):
                value = srcs[n][offset + element_of(x, k)].astype(F32)
                outs[s][n * 4 + k] = (value * root).astype(BF)


def scaled(me, root, parts):
    n = len(parts)
    out = struct((4 * n, NB, NB), BF)
    return pl.pallas_call(
        functools.partial(scaled_kernel, [offset for _, offset in parts]),
        out_shape=[out] * XS,
        in_specs=[pl.BlockSpec(memory_space=pltpu.SMEM)] + vmem_specs(1 + n),
        out_specs=vmem_specs(XS),
        compiler_params=pltpu.CompilerParams(vmem_limit_bytes=16 << 20),
        name="scaled",
    )(me, root, *[array for array, _ in parts])


def grams(me, pieces):
    out = struct((2, NB, NB), BF)
    return pl.pallas_call(
        gram_sorted_kernel,
        out_shape=[struct((2, NB, NB), F32), out, out, out],
        in_specs=[pl.BlockSpec(memory_space=pltpu.SMEM)] + vmem_specs(len(pieces)),
        out_specs=vmem_specs(YS),
        compiler_params=pltpu.CompilerParams(vmem_limit_bytes=16 << 20),
        name="grams",
    )(me, *pieces)


def gram_sorted_kernel(me_ref, *refs):
    srcs, outs = refs[:XS], refs[XS:]
    for t in range(YS):
        y = lax.rem(me_ref[1] + t, YS)
        for k in range(2):
            a = jnp.concatenate([s[y * 2 + k] for s in srcs], axis=1)
            outs[t][k] = (gram(a, a) * (1.0 / NBAND)).astype(outs[t].dtype)


def shifted(array, along, shift):
    step, size = (1, XS) if along == "x" else (XS, YS)
    pairs = []
    for b in range(2 * XS * YS):
        at = b // step % size
        pairs.append((b, b + ((at + shift) % size - at) * step))
    return lax.ppermute(array, "band", pairs)


def exchanged(pieces, along):
    return [pieces[0]] + [shifted(pieces[s], along, s) for s in (1, 2, 3)]


def across(array, senders):
    half = XS * YS
    pairs = [(b, (b + half) % (2 * half)) for b in range(2 * half) if senders(b)]
    return lax.ppermute(array, "band", pairs)


def outer_owner(b):
    return (b // 16 == 0) == (b // 4 % 4 < 2)


def local(coeffs, hamiltonian, adjacency, occupation):
    strip_index = lax.axis_index("strip")
    band_index = lax.axis_index("band")
    count = lax.axis_size("strip")
    ahead = [(i, (i + 1) % count) for i in range(count)]
    back = [(j, i) for i, j in ahead]
    send_up = lambda a: lax.ppermute(a, "strip", ahead)
    send_down = lambda a: lax.ppermute(a, "strip", back)

    low = send_up(coeffs[3 * EY :])
    high = send_down(coeffs[:EY])
    index = block_indices(adjacency, strip_index)
    blocks = hamiltonian.reshape(-1, NB, NB)
    me = jnp.stack([band_index % XS, band_index // XS % YS]).astype(jnp.int32)
    root = jnp.sqrt(occupation).reshape(1, NB)
    c0, cm, c3 = coeffs[:EY], coeffs[EY : 3 * EY], coeffs[3 * EY :]

    m1, part0, part3, far0, far3 = sweep(1, index, [coeffs], blocks)
    u0 = edge(1, part0, far0, low)
    high1 = send_down(u0)
    u3 = edge(1, part3, far3, high)
    low1 = send_up(u3)
    m2, part0, part3 = sweep(2, index, [u0, m1, u3, c0, cm, c3], blocks)
    w3 = edge(2, part3, far3, high1)
    low2 = send_up(w3)
    w0 = edge(2, part0, far0, low1)
    high2 = send_down(w0)
    m3, part0, part3 = sweep(3, index, [w0, m2, w3, u0, m1, u3], blocks)

    inner = grams(me, exchanged(scaled(me, root, [(m3, EY), (m3, 0)]), "x"))
    inner = exchanged(inner, "y")
    inner = sum(a.astype(F32) for a in inner)
    inner_in = across(inner, outer_owner)
    f0 = edge(3, part0, far0, low2)
    f3 = edge(3, part3, far3, high2)
    outer = grams(me, exchanged(scaled(me, root, [(f0, 0), (f3, 0)]), "x"))
    outer = exchanged(outer, "y")
    outer = sum(a.astype(F32) for a in outer)
    outer_in = across(outer, lambda b: not outer_owner(b))
    mine = (band_index // 16 == 0) == (band_index // 4 % 4 < 2)
    return jnp.where(mine, outer + outer_in, inner + inner_in)


def solution(mesh):
    return jax.shard_map(
        local,
        mesh=mesh,
        in_specs=(
            P("strip", None, "band"),
            P("strip", None, None, None),
            P("strip", None),
            P("band"),
        ),
        out_specs=P(("strip", "band"), None, None),
        check_vma=False,
    )
```

```python
import functools

import jax
import jax.numpy as jnp
from jax import lax
from jax.experimental import pallas as pl
from jax.experimental.pallas import tpu as pltpu
from jax.sharding import PartitionSpec as P

EY = 16
EXS = 4
EX = 32
NB = 128
HALF = NB // 2
NBAND = 4096
XS = 4
YS = 4
GROUP = 8
WIDE = GROUP * HALF + 16
THIN = 2 * HALF + 16

BF = jnp.bfloat16
F32 = jnp.float32
VMEM = pltpu.VMEM
LIMIT = 16 << 20
SMEM_SPEC = pl.BlockSpec(memory_space=pltpu.SMEM)
VMEM_SPEC = pl.BlockSpec(memory_space=VMEM)


def struct(shape, dtype):
    return jax.ShapeDtypeStruct(shape, dtype)


def call(kernel, name, outs, scalars, arrays, scratch=(), far=()):
    arrays = [pltpu.with_memory_space_constraint(a, VMEM) for a in arrays]
    arrays += [pltpu.with_memory_space_constraint(a, pltpu.HBM) for a in far]
    return pl.pallas_call(
        kernel,
        out_shape=outs,
        in_specs=[SMEM_SPEC] * len(scalars)
        + [VMEM_SPEC] * (len(arrays) - len(far))
        + [pl.BlockSpec(memory_space=pltpu.HBM)] * len(far),
        out_specs=[VMEM_SPEC] * len(outs),
        scratch_shapes=list(scratch),
        compiler_params=pltpu.CompilerParams(vmem_limit_bytes=LIMIT),
        name=name,
    )(*scalars, *arrays)


def dot(a, b):
    return jnp.dot(a, b, preferred_element_type=F32)


def gram(a, b):
    return lax.dot_general(a, b, (((1,), (1,)), ((), ())), preferred_element_type=F32)


def block_indices(adjacency, strip_index):
    local = jnp.arange(EXS * EY, dtype=jnp.int32)
    row = strip_index * EXS + local // EY
    col = local % EY
    wanted = jnp.stack(
        [
            row * EY + col,
            (row + 1) % EX * EY + col,
            (row + EX - 1) % EX * EY + col,
            row * EY + (col + 1) % EY,
            row * EY + (col + EY - 1) % EY,
        ],
        axis=1,
    )
    hit = adjacency[:, None, :] == wanted[:, :, None]
    slot = jnp.sum(jnp.where(hit, jnp.arange(5, dtype=jnp.int32), 0), axis=2)
    return (local[:, None] * 5 + slot).reshape(-1)


def element_at(x, j):
    return j // 2 * GROUP + 2 * x + j % 2


def pack_groups(me_ref, s_ref, outs):
    row = lax.broadcasted_iota(jnp.int32, (HALF, NB), 0)
    col = lax.broadcasted_iota(jnp.int32, (HALF, NB), 1) - HALF
    tile_row = lax.broadcasted_iota(jnp.int32, (16, NB), 0)
    for s in range(XS):
        x = lax.rem(me_ref[0] + s, XS)

        def element(j, diagonals):
            v = s_ref[element_at(x, j)]
            top, bottom = v[:HALF], v[HALF:]
            low = gram(bottom, v)
            high = gram(top, jnp.concatenate([bottom, top], axis=0))
            packed = jnp.where((col >= 0) & (col < row), high, low)
            outs[s][pl.ds(pl.multiple_of(j * HALF, HALF), HALF), :] = packed.astype(outs[s].dtype)
            diagonal = jnp.sum(jnp.where(col == row, high, 0.0), axis=0, keepdims=True)
            return jnp.where(tile_row == j, diagonal, diagonals)

        diagonals = lax.fori_loop(0, GROUP, element, jnp.zeros((16, NB), F32), unroll=GROUP)
        outs[s][GROUP * HALF :, :] = diagonals.astype(outs[s].dtype)


def group_structs(rows):
    return [struct((rows, NB), F32)] + [struct((rows, NB), BF)] * 3


def sweep_kernel(level, index_ref, *refs):
    if level == 1:
        me_ref, v_ref, root_ref, h_ref, mid_ref, part0, part3, h, sem = refs
        rows = [v_ref.at[pl.ds(r * EY, EY)] for r in range(EXS)]
        before = None
        spans = [pl.ds(r * 5 * EY, 5 * EY) for r in range(EXS)]
        copies = [
            pltpu.make_async_copy(h_ref.at[span], h.at[span], sem.at[r])
            for r, span in enumerate(spans)
        ]
        for copy in copies:
            copy.start()
    elif level == 2:
        v0, vm, v3, p_ref, h, mid_ref, part0, part3 = refs
        rows = [v0, vm.at[pl.ds(0, EY)], vm.at[pl.ds(EY, EY)], v3]
        before = [p_ref.at[pl.ds(r * EY, EY)] for r in range(EXS)]
    else:
        me_ref, root_ref, v0, vm, v3, p0, pm, p3, h, part0, part3, *outs, mid_ref = refs
        rows = [v0, vm.at[pl.ds(0, EY)], vm.at[pl.ds(EY, EY)], v3]
        before = [p0, pm.at[pl.ds(0, EY)], pm.at[pl.ds(EY, EY)], p3]
        root = root_ref[...]
    for r in range(EXS):
        if level == 1:
            copies[r].wait()

        def element(c, carry, r=r):
            at = (r * EY + c) * 5
            right = lax.rem(c + 1, EY)
            left = lax.rem(c + EY - 1, EY)
            terms = [(0, rows[r][c]), (3, rows[r][right]), (4, rows[r][left])]
            if r + 1 < EXS:
                terms.append((1, rows[r + 1][c]))
            if r > 0:
                terms.append((2, rows[r - 1][c]))
            a = jnp.concatenate([h[index_ref[at + k]] for k, _ in terms], axis=1)
            b = jnp.concatenate([v for _, v in terms], axis=0)
            total = dot(a, b)
            if before is not None:
                total = 2.0 * total - before[r][c].astype(F32)
            if r == 0:
                part0[c] = total
            elif r == EXS - 1:
                part3[c] = total
            elif level < 3:
                mid_ref[(r - 1) * EY + c] = total.astype(BF)
            else:
                mid_ref[(2 - r) * EY + c] = (total * root).astype(BF)
            return carry

        lax.fori_loop(0, EY, element, 0, unroll=8)
    if level == 3:
        pack_groups(me_ref, mid_ref, outs)


def sweep(level, scalars, arrays, far=()):
    row = struct((EY, NB, NB), F32)
    mid = (2 * EY, NB, NB)
    outs, scratch = [struct(mid, BF), row, row], []
    if level == 1:
        outs, scratch = outs + [struct(far[0].shape, BF)], [pltpu.SemaphoreType.DMA((EXS,))]
    elif level == 3:
        outs, scratch = [row, row] + group_structs(WIDE), [VMEM(mid, BF)]
    return call(
        functools.partial(sweep_kernel, level), f"sweep{level}", outs, scalars, arrays, scratch, far
    )


def far_term(row, index_ref, h, halo_ref, c):
    base, slot = (0, 2) if row == 0 else ((EXS - 1) * EY, 1)
    return dot(h[index_ref[(base + c) * 5 + slot]], halo_ref[c])


def edge_kernel(level, row, index_ref, part_ref, h, halo_ref, out_ref):
    scale = 1.0 if level == 1 else 2.0

    def element(c, carry):
        out_ref[c] = (part_ref[c] + scale * far_term(row, index_ref, h, halo_ref, c)).astype(BF)
        return carry

    lax.fori_loop(0, EY, element, 0, unroll=8)


def edge(level, row, index, part, h, halo):
    return call(
        functools.partial(edge_kernel, level, row),
        f"edge{level}_{row}",
        [struct((EY, NB, NB), BF)],
        [index],
        [part, h, halo],
    )[0]


def last_kernel(index_ref, me_ref, root_ref, part0, part3, h, low_ref, high_ref, *refs):
    outs, s_ref = refs[:-1], refs[-1]
    root = root_ref[...]
    for row, part, halo, at in ((0, part0, low_ref, 0), (3, part3, high_ref, EY)):

        def element(c, carry):
            value = part[c] + 2.0 * far_term(row, index_ref, h, halo, c)
            s_ref[at + c] = (value * root).astype(BF)
            return carry

        lax.fori_loop(0, EY, element, 0, unroll=8)
    pack_groups(me_ref, s_ref, outs)


def second_kernel(me_ref, *refs):
    pairs, outs = (refs[:XS], refs[XS : 2 * XS]), refs[2 * XS :]
    for n, srcs in enumerate(pairs):
        tail = sum(src[GROUP * HALF :, :].astype(F32) for src in srcs)
        for t in range(YS):
            y = lax.rem(me_ref[1] + t, YS)
            span = pl.ds(pl.multiple_of(y * NB, NB), NB)
            total = sum(src[span, :].astype(F32) for src in srcs)
            at = n * THIN
            outs[t][at : at + NB, :] = total.astype(outs[t].dtype)
            turned = pltpu.roll(tail, lax.rem(16 - 2 * y, 16), 0)
            outs[t][at + NB : at + THIN, :] = turned.astype(outs[t].dtype)


def third_kernel(me_ref, *refs):
    srcs, (own_ref, sent_ref) = refs[:YS], refs[YS:]
    own = pl.ds(pl.multiple_of(me_ref[2] * THIN, 16), THIN)
    other = pl.ds(pl.multiple_of((1 - me_ref[2]) * THIN, 16), THIN)
    own_ref[...] = sum(src[own, :].astype(F32) for src in srcs)
    sent_ref[...] = sum(src[other, :].astype(F32) for src in srcs).astype(BF)


def final_kernel(own_ref, received_ref, out_ref):
    row = lax.broadcasted_iota(jnp.int32, (HALF, HALF), 0)
    col = lax.broadcasted_iota(jnp.int32, (HALF, HALF), 1)
    total = (own_ref[...] + received_ref[...].astype(F32)) * (1.0 / NBAND)
    for k in range(2):
        u = total[k * HALF : (k + 1) * HALF]
        b, w = u[:, :HALF], u[:, HALF:]
        turned = u.T
        b_t, w_t = turned[:HALF], turned[HALF:]
        diagonal = total[NB + k : NB + k + 1, HALF:]
        a = jnp.where(col < row, w, w_t)
        a = jnp.where(col == row, diagonal, a)
        c = jnp.where(col >= row, w, w_t)
        out_ref[k, :HALF, :] = jnp.concatenate([a, b_t], axis=1)
        out_ref[k, HALF:, :] = jnp.concatenate([b, c], axis=1)


def shifted(array, along, shift):
    step, size = (1, XS) if along == "x" else (XS, YS)
    pairs = []
    for b in range(2 * XS * YS):
        at = b // step % size
        pairs.append((b, b + ((at + shift) % size - at) * step))
    return lax.ppermute(array, "band", pairs)


def exchanged(pieces, along):
    return [pieces[0]] + [shifted(pieces[s], along, s) for s in (1, 2, 3)]


def across(array):
    half = XS * YS
    return lax.ppermute(array, "band", [(b, (b + half) % (2 * half)) for b in range(2 * half)])


def local(coeffs, hamiltonian, adjacency, occupation):
    strip_index = lax.axis_index("strip")
    band_index = lax.axis_index("band")
    count = lax.axis_size("strip")
    ahead = [(i, (i + 1) % count) for i in range(count)]
    back = [(j, i) for i, j in ahead]
    send_up = lambda a: lax.ppermute(a, "strip", ahead)
    send_down = lambda a: lax.ppermute(a, "strip", back)

    low = send_up(coeffs[3 * EY :])
    high = send_down(coeffs[:EY])
    index = block_indices(adjacency, strip_index)
    h = hamiltonian.reshape(-1, NB, NB)
    outer_owner = 1 - ((band_index >> 4) ^ (band_index >> 3 & 1))
    me = jnp.stack([band_index & 3, band_index >> 2 & 3, outer_owner])
    root = jnp.sqrt(occupation).reshape(1, NB)

    m1, part0, part3, h = sweep(1, [index, me], [coeffs, root], [h])
    u0 = edge(1, 0, index, part0, h, low)
    high1 = send_down(u0)
    u3 = edge(1, 3, index, part3, h, high)
    low1 = send_up(u3)
    m2, part0, part3 = sweep(2, [index], [u0, m1, u3, coeffs, h])
    w3 = edge(2, 3, index, part3, h, high1)
    low2 = send_up(w3)
    w0 = edge(2, 0, index, part0, h, low1)
    high2 = send_down(w0)
    part0, part3, *inner = sweep(3, [index, me], [root, w0, m2, w3, u0, m1, u3, h])
    inner = exchanged(inner, "x")
    outer = call(
        last_kernel,
        "last",
        group_structs(WIDE),
        [index, me],
        [root, part0, part3, h, low2, high2],
        [VMEM((2 * EY, NB, NB), BF)],
    )
    outer = exchanged(outer, "x")
    both = call(second_kernel, "second", group_structs(2 * THIN), [me], [*inner, *outer])
    own, sent = call(
        third_kernel,
        "third",
        [struct((THIN, NB), F32), struct((THIN, NB), BF)],
        [me],
        exchanged(both, "y"),
    )
    return call(final_kernel, "final", [struct((2, NB, NB), F32)], [], [own, across(sent)])[0]


def solution(mesh):
    return jax.shard_map(
        local,
        mesh=mesh,
        in_specs=(
            P("strip", None, "band"),
            P("strip", None, None, None),
            P("strip", None),
            P("band"),
        ),
        out_specs=P(("strip", "band"), None, None),
        check_vma=False,
    )
```

```python
import functools

import jax
import jax.numpy as jnp
from jax import lax
from jax.experimental import pallas as pl
from jax.experimental.pallas import tpu as pltpu
from jax.sharding import PartitionSpec as P


EY = 16
EXS = 4
EX = 32
NB = 128
HALF = NB // 2
NBAND = 4096
XS = 4
YS = 4
PART = EY // 2
PAIR = 2 * HALF
WIDE = 8 * HALF + 16
THIN = PAIR + 16

BF = jnp.bfloat16
F32 = jnp.float32
VMEM = pltpu.VMEM
LIMIT = 16 << 20
RUN = PART * 5
SMEM_SPEC = pl.BlockSpec(memory_space=pltpu.SMEM)
VMEM_SPEC = pl.BlockSpec(memory_space=VMEM)

FAR, NEAR = 0, 3
SELF, INWARD, OUTWARD, RIGHT, LEFT = range(5)


def struct(shape, dtype):
    return jax.ShapeDtypeStruct(shape, dtype)


def call(kernel, outs, scalars, arrays, scratch=(), out_specs=None, hbm=()):
    arrays = [pltpu.with_memory_space_constraint(a, VMEM) for a in arrays]
    return pl.pallas_call(
        kernel,
        out_shape=outs,
        in_specs=[SMEM_SPEC] * len(scalars)
        + [VMEM_SPEC] * len(arrays)
        + [pl.BlockSpec(memory_space=pltpu.HBM)] * len(hbm),
        out_specs=out_specs or [VMEM_SPEC] * len(outs),
        scratch_shapes=list(scratch),
        compiler_params=pltpu.CompilerParams(vmem_limit_bytes=LIMIT),
    )(*scalars, *arrays, *[pltpu.with_memory_space_constraint(a, pltpu.HBM) for a in hbm])


def dot(a, b):
    return jnp.dot(a, b, preferred_element_type=F32)


def gram(a, b):
    return lax.dot_general(a, b, (((1,), (1,)), ((), ())), preferred_element_type=F32)


def odd():
    return lax.axis_index("strip") & 1


def place(stage):
    band = lax.axis_index("band")
    x, y = band & 3, band >> 2 & 3
    return jnp.where(odd() == stage, x, y)


def row_base(row):
    return (row + odd() * (EXS - 1 - 2 * row)) * EY


def start_kernel(c_ref, fa_ref, fb_ref, near_ref, sem):
    far, near = row_base(FAR), row_base(NEAR)
    copies = [
        pltpu.make_async_copy(c_ref.at[pl.ds(at, size)], ref, sem.at[n])
        for n, (at, size, ref) in enumerate(
            ((far, PART, fa_ref), (far + PART, PART, fb_ref), (near, EY, near_ref))
        )
    ]
    for copy in copies:
        copy.start()
    for copy in copies:
        copy.wait()


def fill_places(adj_ref, table):
    local = lax.broadcasted_iota(jnp.int32, (1, EXS * EY), 1)
    row = lax.axis_index("strip") * EXS + (local >> 4)
    col = local & (EY - 1)
    inward = 1 - 2 * odd()
    wanted = {
        SELF: (row, col),
        INWARD: (row + inward & EX - 1, col),
        OUTWARD: (row - inward & EX - 1, col),
        RIGHT: (row, col + 1 & EY - 1),
        LEFT: (row, col - 1 & EY - 1),
    }
    for k, (r, c) in wanted.items():
        slot = sum(jnp.where(adj_ref[j : j + 1, :] == r * EY + c, j, 0) for j in range(1, 5))
        table[k : k + 1, : EXS * EY] = local * 5 + slot


def pack(v, ref, at):
    row = lax.broadcasted_iota(jnp.int32, (HALF, NB), 0)
    col = lax.broadcasted_iota(jnp.int32, (HALF, NB), 1) - HALF
    top, bottom = v[:HALF], v[HALF:]
    low = gram(bottom, v)
    high = gram(top, jnp.concatenate([bottom, top], axis=0))
    packed = jnp.where((col >= 0) & (col < row), high, low)
    ref[at * HALF : (at + 1) * HALF, :] = packed.astype(ref.dtype)
    return jnp.sum(jnp.where(col == row, high, 0.0), axis=0, keepdims=True)


def pack_groups(s_ref, outs):
    tile_row = lax.broadcasted_iota(jnp.int32, (16, NB), 0)
    turn, me = odd(), place(0)
    for s in range(XS):
        to = me ^ s
        diagonals = jnp.zeros((16, NB), F32)
        for j in range(8):
            at = jnp.where(turn == 1, to * 8 + j, j // 2 * 8 + 2 * to + j % 2)
            diagonals = jnp.where(tile_row == j, pack(s_ref[at], outs[s], j), diagonals)
        outs[s][8 * HALF :, :] = diagonals.astype(outs[s].dtype)


def group_structs(rows):
    return [struct((rows, NB), F32)] + [struct((rows, NB), BF)] * 3


def apply_row(row, first, count, index_ref, h, value, past, halo, put):
    base = row_base(row)

    def element(n, carry):
        c = first + n
        terms = [
            (SELF, value(row, c)),
            (RIGHT, value(row, c + 1 & EY - 1)),
            (LEFT, value(row, c - 1 & EY - 1)),
        ]
        if row < NEAR:
            terms.append((INWARD, value(row + 1, c)))
        elif halo is not None:
            terms.append((INWARD, halo[c]))
        if row > FAR:
            terms.append((OUTWARD, value(row - 1, c)))
        a = jnp.concatenate([h[index_ref[k, base + c]] for k, _ in terms], axis=1)
        b = jnp.concatenate([v for _, v in terms], axis=0)
        total = dot(a, b)
        if past is not None:
            total = 2.0 * total - past(row, c).astype(F32)
        put(c, total)
        return carry

    lax.fori_loop(0, count, element, 0, unroll=PART)


def putter(ref, root=None):
    def put(c, total):
        ref[c] = (total if root is None else total * root).astype(ref.dtype)

    return put


def first_kernel(adj_hbm, occ_hbm, c_ref, h_ref, *refs):
    index_ref, root_ref, part_ref, x_ref, y_ref, near_ref, v_ref, h, adj, occ, table, sem = refs
    small = [
        pltpu.make_async_copy(adj_hbm, adj, sem.at[0]),
        pltpu.make_async_copy(occ_hbm, occ, sem.at[1]),
    ]
    place = pltpu.make_async_copy(table, index_ref, sem.at[2])
    fields, runs = [], []
    for row in range(EXS):
        span = pl.ds(row_base(row), EY)
        fields.append(pltpu.make_async_copy(c_ref.at[span], v_ref.at[span], sem.at[3 + row]))
        for n in range(2):
            span = pl.ds(row_base(row) * 5 + n * RUN, RUN)
            at = 3 + EXS + len(runs)
            runs.append(pltpu.make_async_copy(h_ref.at[span], h.at[span], sem.at[at]))
    order = small + fields[:2] + runs[:2]
    for row in range(1, EXS):
        order += fields[row + 1 : row + 2] + runs[2 * row : 2 * row + 2]
    for copy in order:
        copy.start()
    for copy in small:
        copy.wait()
    fill_places(adj, table)
    place.start()
    root_ref[...] = jnp.sqrt(occ[...])
    place.wait()
    fields[0].wait()
    value = lambda row, c: v_ref[row_base(row) + c]
    for row, out in enumerate((part_ref, x_ref, y_ref, near_ref)):
        if row < NEAR:
            fields[row + 1].wait()
        for n in range(2):
            runs[2 * row + n].wait()
            apply_row(row, n * PART, PART, index_ref, h, value, None, None, putter(out))


def inner_kernel(rows, index_ref, x, y, near, halo, h, *refs):
    past_ref, *outs = refs
    value = lambda row, c: (None, x, y, near)[row][c]
    past = lambda row, c: past_ref[row_base(row) + c]
    for row, out in zip(rows, outs):
        apply_row(row, 0, EY, index_ref, h, value, past, halo, putter(out))


def second_sweep_kernel(index_ref, fa, fb, x, y, near, h, past_ref, part_ref, x_out, y_out, far):
    far[:PART] = fa[...]
    far[PART:] = fb[...]
    value = lambda row, c: (far, x, y, near)[row][c]
    past = lambda row, c: past_ref[row_base(row) + c]
    for row, out in enumerate((part_ref, x_out, y_out)):
        apply_row(row, 0, EY, index_ref, h, value, past, None, putter(out))


def early_kernel(index_ref, root_ref, x, y, near, halo, h, past_y, past_near, *refs):
    outs, s_ref = refs[:-1], refs[-1]
    root = root_ref[...]
    value = lambda row, c: (None, x, y, near)[row][c]
    past = lambda row, c: (None, None, past_y, past_near)[row][c]
    for row, at in ((2, odd()), (NEAR, 1 - odd())):
        put = putter(s_ref.at[pl.ds(at * EY, EY)], root)
        apply_row(row, 0, EY, index_ref, h, value, past, halo, put)
    pack_groups(s_ref, outs)


def third_sweep_kernel(index_ref, root_ref, fa, fb, x, y, h, pa, pb, px, part_ref, x_out, far, pfar):
    far[:PART] = fa[...]
    far[PART:] = fb[...]
    pfar[:PART] = pa[...]
    pfar[PART:] = pb[...]
    root = root_ref[...]
    value = lambda row, c: (far, x, y)[row][c]
    past = lambda row, c: (pfar, px)[row][c]
    for row, out in ((FAR, putter(part_ref)), (1, putter(x_out, root))):
        apply_row(row, 0, EY, index_ref, h, value, past, None, out)


def last_kernel(index_ref, root_ref, part_ref, h, halo_a, halo_b, x, *refs):
    outs, s_ref = refs[:-1], refs[-1]
    root = root_ref[...]
    base = row_base(FAR)
    at = odd() * EY
    s_ref[pl.ds(EY - at, EY)] = x[...]
    for first, halo in ((0, halo_a), (PART, halo_b)):
        for c in range(PART):
            term = dot(h[index_ref[OUTWARD, base + first + c]], halo[c])
            s_ref[at + first + c] = ((part_ref[first + c] + 2.0 * term) * root).astype(BF)
    pack_groups(s_ref, outs)


def edge_kernel(level, row, first, index_ref, part_ref, h, halo_ref, out_ref):
    scale = 1.0 if level == 1 else 2.0
    way = OUTWARD if row == FAR else INWARD
    base = row_base(row) + first
    for c in range(out_ref.shape[0]):
        term = dot(h[index_ref[way, base + c]], halo_ref[c])
        out_ref[c] = (part_ref[first + c] + scale * term).astype(BF)


def edge(level, row, first, index, part, h, halo):
    return call(
        functools.partial(edge_kernel, level, row, first),
        [struct(halo.shape, BF)],
        [index],
        [part, h, halo],
    )[0]


def second_kernel(*refs):
    pairs, outs = (refs[:XS], refs[XS : 2 * XS]), refs[2 * XS :]
    me = place(1)
    for n, srcs in enumerate(pairs):
        tail = sum(src[8 * HALF :, :].astype(F32) for src in srcs)
        at = n * THIN
        for t in range(YS):
            to = me ^ t
            span = pl.ds(pl.multiple_of(to * PAIR, PAIR), PAIR)
            total = sum(src[span, :].astype(F32) for src in srcs)
            outs[t][at : at + PAIR, :] = total.astype(outs[t].dtype)
            turned = pltpu.roll(tail, lax.rem(16 - 2 * to, 16), 0)
            outs[t][at + PAIR : at + THIN, :] = turned.astype(outs[t].dtype)


def third_kernel(*refs):
    srcs, (own_ref, sent_ref) = refs[:YS], refs[YS:]
    own_late = 1 - (lax.axis_index("band") >> 4 ^ odd())
    own = pl.ds(pl.multiple_of(own_late * THIN, 16), THIN)
    other = pl.ds(pl.multiple_of((1 - own_late) * THIN, 16), THIN)
    own_ref[...] = sum(src[own, :].astype(F32) for src in srcs)
    sent_ref[...] = sum(src[other, :].astype(F32) for src in srcs).astype(BF)


def final_kernel(own_ref, received_ref, out_ref):
    row = lax.broadcasted_iota(jnp.int32, (HALF, HALF), 0)
    col = lax.broadcasted_iota(jnp.int32, (HALF, HALF), 1)
    total = (own_ref[...] + received_ref[...].astype(F32)) * (1.0 / NBAND)
    for k in range(2):
        u = total[k * HALF : (k + 1) * HALF]
        b, w = u[:, :HALF], u[:, HALF:]
        turned = u.T
        b_t, w_t = turned[:HALF], turned[HALF:]
        diagonal = total[PAIR + k : PAIR + k + 1, HALF:]
        a = jnp.where(col < row, w, w_t)
        a = jnp.where(col == row, diagonal, a)
        c = jnp.where(col >= row, w, w_t)
        out_ref[k, :HALF, :] = jnp.concatenate([a, b_t], axis=1)
        out_ref[k, HALF:, :] = jnp.concatenate([b, c], axis=1)


def exchanged(pieces, stage):
    bands, strips = lax.axis_size("band"), lax.axis_size("strip")
    arrived = [pieces[0]]
    for s in (2, 1, 3):
        pairs = []
        for strip in range(strips):
            step = 1 if strip % 2 == stage else XS
            pairs += [(b * strips + strip, (b ^ s * step) * strips + strip) for b in range(bands)]
        arrived.append(lax.ppermute(pieces[s], ("band", "strip"), pairs))
    return arrived


def across(array):
    half = XS * YS
    return lax.ppermute(array, "band", [(b, (b + half) % (2 * half)) for b in range(2 * half)])


def swapped(array, first):
    count = lax.axis_size("strip")
    pairs = []
    for i in range(first, first + count, 2):
        a, b = i % count, (i + 1) % count
        pairs += [(a, b), (b, a)]
    return lax.ppermute(array, "strip", pairs)


def stage(kernel, outs, scalars, arrays, *more, **options):
    return call(kernel, outs, scalars, arrays, *more, **options)


def program(coeffs, hamiltonian, adjacency, occupation):
    h = hamiltonian.reshape(-1, NB, NB)
    row, part = struct((EY, NB, NB), BF), struct((PART, NB, NB), BF)
    wide = struct((EY, NB, NB), F32)
    scratch = VMEM(row.shape, BF)
    fa, fb, near = stage(
        start_kernel, [part, part, row], [], [], [pltpu.SemaphoreType.DMA((3,))], hbm=[coeffs]
    )
    fa_in, fb_in = swapped(fa, 1), swapped(fb, 1)
    near_in = swapped(near, 0)
    table = struct((8, NB), jnp.int32)
    outs = [table, struct((1, NB), F32), wide, row, row, wide, struct(coeffs.shape, BF)]
    index, root, far, x1, y1, near, field, h = stage(
        first_kernel,
        outs + [struct(h.shape, BF)],
        [],
        [],
        [
            VMEM((5, EXS * EY), jnp.int32),
            VMEM((1, NB), F32),
            VMEM(table.shape, jnp.int32),
            pltpu.SemaphoreType.DMA((3 + 3 * EXS,)),
        ],
        [SMEM_SPEC] + [VMEM_SPEC] * len(outs),
        hbm=[adjacency.T, occupation.reshape(1, NB), coeffs, h],
    )
    near1 = edge(1, NEAR, 0, index, near, h, near_in)
    near_in = swapped(near1, 0)
    fa1 = edge(1, FAR, 0, index, far, h, fa_in)
    fa_in = swapped(fa1, 1)
    fb1 = edge(1, FAR, PART, index, far, h, fb_in)
    fb_in = swapped(fb1, 1)
    inner = functools.partial(inner_kernel, (NEAR,))
    (near2,) = stage(inner, [row], [index], [x1, y1, near1, near_in, h, field])
    near_in = swapped(near2, 0)
    far, x2, y2 = stage(
        second_sweep_kernel,
        [wide, row, row],
        [index],
        [fa1, fb1, x1, y1, near1, h, field],
        [scratch],
    )
    fa2 = edge(2, FAR, 0, index, far, h, fa_in)
    fa_in = swapped(fa2, 1)
    early = stage(
        early_kernel,
        group_structs(WIDE),
        [index],
        [root, x2, y2, near2, near_in, h, y1, near1],
        [VMEM((2 * EY, NB, NB), BF)],
    )
    fb2 = edge(2, FAR, PART, index, far, h, fb_in)
    fb_in = swapped(fb2, 1)
    early = exchanged(early, 0)
    far, x = stage(
        third_sweep_kernel,
        [wide, row],
        [index],
        [root, fa2, fb2, x2, y2, h, fa1, fb1, x1],
        [scratch, scratch],
    )
    late = stage(
        last_kernel,
        group_structs(WIDE),
        [index],
        [root, far, h, fa_in, fb_in, x],
        [VMEM((2 * EY, NB, NB), BF)],
    )
    late = exchanged(late, 0)
    both = stage(second_kernel, group_structs(2 * THIN), [], [*early, *late])
    thin = [struct((THIN, NB), F32), struct((THIN, NB), BF)]
    own, sent = stage(third_kernel, thin, [], exchanged(both, 1))
    return stage(final_kernel, [struct((2, NB, NB), F32)], [], [own, across(sent)])[0]


def solution(mesh):
    return jax.shard_map(
        program,
        mesh=mesh,
        in_specs=(
            P("strip", None, "band"),
            P("strip", None, None, None),
            P("strip", None),
            P("band"),
        ),
        out_specs=P(("strip", "band"), None, None),
        check_vma=False,
    )
```

```python
import functools

import jax
import jax.numpy as jnp
from jax import lax
from jax.experimental import pallas as pl
from jax.experimental.pallas import tpu as pltpu
from jax.sharding import PartitionSpec as P


EY = 16
EXS = 4
EX = 32
NB = 128
HALF = NB // 2
NBAND = 4096
XS = 4
YS = 4
PART = EY // 2
PAIR = 2 * HALF
WIDE = 8 * HALF + 16
THIN = PAIR + 16

BF = jnp.bfloat16
F32 = jnp.float32
VMEM = pltpu.VMEM
LIMIT = 16 << 20
RUN = PART * 5
SMEM_SPEC = pl.BlockSpec(memory_space=pltpu.SMEM)
VMEM_SPEC = pl.BlockSpec(memory_space=VMEM)

FAR, NEAR = 0, 3
SELF, INWARD, OUTWARD, RIGHT, LEFT = range(5)


def struct(shape, dtype):
    return jax.ShapeDtypeStruct(shape, dtype)


def call(kernel, outs, scalars, arrays, scratch=(), hbm=(), limit=LIMIT):
    arrays = [pltpu.with_memory_space_constraint(a, VMEM) for a in arrays]
    return pl.pallas_call(
        kernel,
        out_shape=outs,
        in_specs=[SMEM_SPEC] * len(scalars)
        + [VMEM_SPEC] * len(arrays)
        + [pl.BlockSpec(memory_space=pltpu.HBM)] * len(hbm),
        out_specs=[VMEM_SPEC] * len(outs),
        scratch_shapes=list(scratch),
        compiler_params=pltpu.CompilerParams(vmem_limit_bytes=limit),
    )(*scalars, *arrays, *[pltpu.with_memory_space_constraint(a, pltpu.HBM) for a in hbm])


def dot(a, b):
    return jnp.dot(a, b, preferred_element_type=F32)


def gram(a, b):
    return lax.dot_general(a, b, (((1,), (1,)), ((), ())), preferred_element_type=F32)


def odd():
    return lax.axis_index("strip") & 1


def place(stage):
    band = lax.axis_index("band")
    x, y = band & 3, band >> 2 & 3
    return jnp.where(odd() == stage, x, y)


def row_base(row):
    return (row + odd() * (EXS - 1 - 2 * row)) * EY


def start_kernel(c_ref, fa_ref, fb_ref, near_ref, sem):
    far, near = row_base(FAR), row_base(NEAR)
    copies = [
        pltpu.make_async_copy(c_ref.at[pl.ds(at, size)], ref, sem.at[n])
        for n, (at, size, ref) in enumerate(
            ((far, PART, fa_ref), (far + PART, PART, fb_ref), (near, EY, near_ref))
        )
    ]
    for copy in copies:
        copy.start()
    for copy in copies:
        copy.wait()


def fill_places(adj_ref, table):
    local = lax.broadcasted_iota(jnp.int32, (1, EXS * EY), 1)
    row = lax.axis_index("strip") * EXS + (local >> 4)
    col = local & (EY - 1)
    inward = 1 - 2 * odd()
    wanted = {
        SELF: (row, col),
        INWARD: (row + inward & EX - 1, col),
        OUTWARD: (row - inward & EX - 1, col),
        RIGHT: (row, col + 1 & EY - 1),
        LEFT: (row, col - 1 & EY - 1),
    }
    for k, (r, c) in wanted.items():
        slot = sum(jnp.where(adj_ref[j : j + 1, :] == r * EY + c, j, 0) for j in range(1, 5))
        table[k : k + 1, : EXS * EY] = local * 5 + slot


def pack(v, ref, at):
    row = lax.broadcasted_iota(jnp.int32, (HALF, NB), 0)
    col = lax.broadcasted_iota(jnp.int32, (HALF, NB), 1) - HALF
    product = gram(v, v)
    low, high = product[HALF:], pltpu.roll(product[:HALF], HALF, 1)
    packed = jnp.where((col >= 0) & (col < row), high, low)
    ref[at * HALF : (at + 1) * HALF, :] = packed.astype(ref.dtype)
    return jnp.sum(jnp.where(col == row, high, 0.0), axis=0, keepdims=True)


def pack_groups(s_ref, outs):
    tile_row = lax.broadcasted_iota(jnp.int32, (16, NB), 0)
    turn, me = odd(), place(0)
    for s in range(XS):
        to = me ^ s
        diagonals = jnp.zeros((16, NB), F32)
        for j in range(8):
            at = jnp.where(turn == 1, to * 8 + j, j // 2 * 8 + 2 * to + j % 2)
            diagonals = jnp.where(tile_row == j, pack(s_ref[at], outs[s], j), diagonals)
        outs[s][8 * HALF :, :] = diagonals.astype(outs[s].dtype)


def group_structs(rows):
    return [struct((rows, NB), F32)] + [struct((rows, NB), BF)] * 3


def apply_row(row, first, count, block, value, past, halo, put):
    base = row_base(row)

    def element(n, carry):
        c = first + n
        terms = [
            (SELF, value(row, c)),
            (RIGHT, value(row, c + 1 & EY - 1)),
            (LEFT, value(row, c - 1 & EY - 1)),
        ]
        if row < NEAR:
            terms.append((INWARD, value(row + 1, c)))
        elif halo is not None:
            terms.append((INWARD, halo[c]))
        if row > FAR:
            terms.append((OUTWARD, value(row - 1, c)))
        a = jnp.concatenate([block(base + c, k) for k, _ in terms], axis=1)
        b = jnp.concatenate([v for _, v in terms], axis=0)
        total = dot(a, b)
        if past is not None:
            total = 2.0 * total - past(row, c).astype(F32)
        put(c, total)
        return carry

    lax.fori_loop(0, count, element, 0, unroll=PART)


def sorted_block(h):
    return lambda e, k: h[e * 5 + k]


def putter(ref, root=None):
    def put(c, total):
        ref[c] = (total if root is None else total * root).astype(ref.dtype)

    return put


def first_kernel(adj_hbm, occ_hbm, c_ref, h_ref, *refs):
    root_ref, part_ref, x_ref, y_ref, near_ref, v_ref, sorted_ref, *refs = refs
    h, index_ref, adj, occ, table, sem = refs
    small = [
        pltpu.make_async_copy(adj_hbm, adj, sem.at[0]),
        pltpu.make_async_copy(occ_hbm, occ, sem.at[1]),
    ]
    place = pltpu.make_async_copy(table, index_ref, sem.at[2])
    fields, runs = [], []
    for row in range(EXS):
        span = pl.ds(row_base(row), EY)
        fields.append(pltpu.make_async_copy(c_ref.at[span], v_ref.at[span], sem.at[3 + row]))
        for n in range(2):
            span = pl.ds(row_base(row) * 5 + n * RUN, RUN)
            at = 3 + EXS + len(runs)
            runs.append(pltpu.make_async_copy(h_ref.at[span], h.at[span], sem.at[at]))
    order = small + fields[:2] + runs[:2]
    for row in range(1, EXS):
        order += fields[row + 1 : row + 2] + runs[2 * row : 2 * row + 2]
    for copy in order:
        copy.start()
    for copy in small:
        copy.wait()
    fill_places(adj, table)
    place.start()
    root_ref[...] = jnp.sqrt(occ[...])
    place.wait()
    fields[0].wait()
    value = lambda row, c: v_ref[row_base(row) + c]

    def block(e, k):
        found = h[index_ref[k, e]]
        sorted_ref[e * 5 + k] = found
        return found

    for row, out in enumerate((part_ref, x_ref, y_ref, near_ref)):
        if row < NEAR:
            fields[row + 1].wait()
        for n in range(2):
            runs[2 * row + n].wait()
            apply_row(row, n * PART, PART, block, value, None, None, putter(out))
            for c in range(n * PART, (n + 1) * PART):
                if row == FAR:
                    block(row_base(row) + c, OUTWARD)
                if row == NEAR:
                    block(row_base(row) + c, INWARD)


def inner_kernel(rows, x, y, near, halo, h, *refs):
    past_ref, *outs = refs
    value = lambda row, c: (None, x, y, near)[row][c]
    past = lambda row, c: past_ref[row_base(row) + c]
    for row, out in zip(rows, outs):
        apply_row(row, 0, EY, sorted_block(h), value, past, halo, putter(out))


def second_sweep_kernel(fa, fb, x, y, near, h, past_ref, part_ref, x_out, y_out, far):
    far[:PART] = fa[...]
    far[PART:] = fb[...]
    value = lambda row, c: (far, x, y, near)[row][c]
    past = lambda row, c: past_ref[row_base(row) + c]
    for row, out in enumerate((part_ref, x_out, y_out)):
        apply_row(row, 0, EY, sorted_block(h), value, past, None, putter(out))


def early_kernel(root_ref, x, y, near, halo, h, past_y, past_near, *refs):
    outs, s_ref = refs[:-1], refs[-1]
    root = root_ref[...]
    value = lambda row, c: (None, x, y, near)[row][c]
    past = lambda row, c: (None, None, past_y, past_near)[row][c]
    for row, at in ((2, odd()), (NEAR, 1 - odd())):
        put = putter(s_ref.at[pl.ds(at * EY, EY)], root)
        apply_row(row, 0, EY, sorted_block(h), value, past, halo, put)
    pack_groups(s_ref, outs)


def third_sweep_kernel(root_ref, fa, fb, x, y, h, pa, pb, px, part_ref, x_out, far, pfar):
    far[:PART] = fa[...]
    far[PART:] = fb[...]
    pfar[:PART] = pa[...]
    pfar[PART:] = pb[...]
    root = root_ref[...]
    value = lambda row, c: (far, x, y)[row][c]
    past = lambda row, c: (pfar, px)[row][c]
    for row, out in ((FAR, putter(part_ref)), (1, putter(x_out, root))):
        apply_row(row, 0, EY, sorted_block(h), value, past, None, out)


def last_kernel(root_ref, part_ref, h, halo_a, halo_b, x, *refs):
    outs, s_ref = refs[:-1], refs[-1]
    root = root_ref[...]
    base = row_base(FAR)
    at = odd() * EY
    s_ref[pl.ds(EY - at, EY)] = x[...]
    for first, halo in ((0, halo_a), (PART, halo_b)):
        for c in range(PART):
            term = dot(h[(base + first + c) * 5 + OUTWARD], halo[c])
            s_ref[at + first + c] = ((part_ref[first + c] + 2.0 * term) * root).astype(BF)
    pack_groups(s_ref, outs)


def edge_kernel(level, row, first, part_ref, h, halo_ref, out_ref):
    scale = 1.0 if level == 1 else 2.0
    way = OUTWARD if row == FAR else INWARD
    base = row_base(row) + first
    for c in range(out_ref.shape[0]):
        term = dot(h[(base + c) * 5 + way], halo_ref[c])
        out_ref[c] = (part_ref[first + c] + scale * term).astype(BF)


def edge(level, row, first, part, h, halo):
    return call(
        functools.partial(edge_kernel, level, row, first),
        [struct(halo.shape, BF)],
        [],
        [part, h, halo],
    )[0]


def second_kernel(*refs):
    pairs, outs = (refs[:XS], refs[XS : 2 * XS]), refs[2 * XS :]
    me = place(1)
    for n, srcs in enumerate(pairs):
        tail = sum(src[8 * HALF :, :].astype(F32) for src in srcs)
        at = n * THIN
        for t in range(YS):
            to = me ^ t
            span = pl.ds(pl.multiple_of(to * PAIR, PAIR), PAIR)
            total = sum(src[span, :].astype(F32) for src in srcs)
            outs[t][at : at + PAIR, :] = total.astype(outs[t].dtype)
            turned = pltpu.roll(tail, lax.rem(16 - 2 * to, 16), 0)
            outs[t][at + PAIR : at + THIN, :] = turned.astype(outs[t].dtype)


def third_kernel(*refs):
    srcs, (own_ref, sent_ref) = refs[:YS], refs[YS:]
    own_late = 1 - (lax.axis_index("band") >> 4 ^ odd())
    own = pl.ds(pl.multiple_of(own_late * THIN, 16), THIN)
    other = pl.ds(pl.multiple_of((1 - own_late) * THIN, 16), THIN)
    own_ref[...] = sum(src[own, :].astype(F32) for src in srcs)
    sent_ref[...] = sum(src[other, :].astype(F32) for src in srcs).astype(BF)


def final_kernel(own_ref, received_ref, out_ref):
    row = lax.broadcasted_iota(jnp.int32, (HALF, HALF), 0)
    col = lax.broadcasted_iota(jnp.int32, (HALF, HALF), 1)
    total = (own_ref[...] + received_ref[...].astype(F32)) * (1.0 / NBAND)
    for k in range(2):
        u = total[k * HALF : (k + 1) * HALF]
        b, w = u[:, :HALF], u[:, HALF:]
        turned = u.T
        b_t, w_t = turned[:HALF], turned[HALF:]
        diagonal = total[PAIR + k : PAIR + k + 1, HALF:]
        a = jnp.where(col < row, w, w_t)
        a = jnp.where(col == row, diagonal, a)
        c = jnp.where(col >= row, w, w_t)
        out_ref[k, :HALF, :] = jnp.concatenate([a, b_t], axis=1)
        out_ref[k, HALF:, :] = jnp.concatenate([b, c], axis=1)


def exchanged(pieces, stage):
    bands, strips = lax.axis_size("band"), lax.axis_size("strip")
    arrived = [pieces[0]]
    for s in (2, 1, 3):
        pairs = []
        for strip in range(strips):
            step = 1 if strip % 2 == stage else XS
            pairs += [(b * strips + strip, (b ^ s * step) * strips + strip) for b in range(bands)]
        arrived.append(lax.ppermute(pieces[s], ("band", "strip"), pairs))
    return arrived


def across(array):
    half = XS * YS
    return lax.ppermute(array, "band", [(b, (b + half) % (2 * half)) for b in range(2 * half)])


def swapped(array, first):
    count = lax.axis_size("strip")
    pairs = []
    for i in range(first, first + count, 2):
        a, b = i % count, (i + 1) % count
        pairs += [(a, b), (b, a)]
    return lax.ppermute(array, "strip", pairs)


def stage(kernel, outs, scalars, arrays, *more, **options):
    return call(kernel, outs, scalars, arrays, *more, **options)


def program(coeffs, hamiltonian, adjacency, occupation):
    h = hamiltonian.reshape(-1, NB, NB)
    row, part = struct((EY, NB, NB), BF), struct((PART, NB, NB), BF)
    wide = struct((EY, NB, NB), F32)
    scratch = VMEM(row.shape, BF)
    fa, fb, near = stage(
        start_kernel, [part, part, row], [], [], [pltpu.SemaphoreType.DMA((3,))], hbm=[coeffs]
    )
    fa_in, fb_in = swapped(fa, 1), swapped(fb, 1)
    near_in = swapped(near, 0)
    table = struct((8, NB), jnp.int32)
    outs = [struct((1, NB), F32), wide, row, row, wide, struct(coeffs.shape, BF)]
    root, far, x1, y1, near, field, h = stage(
        first_kernel,
        outs + [struct(h.shape, BF)],
        [],
        [],
        [
            VMEM(h.shape, BF),
            pltpu.SMEM(table.shape, jnp.int32),
            VMEM((5, EXS * EY), jnp.int32),
            VMEM((1, NB), F32),
            VMEM(table.shape, jnp.int32),
            pltpu.SemaphoreType.DMA((3 + 3 * EXS,)),
        ],
        limit=32 << 20,
        hbm=[adjacency.T, occupation.reshape(1, NB), coeffs, h],
    )
    near1 = edge(1, NEAR, 0, near, h, near_in)
    near_in = swapped(near1, 0)
    fa1 = edge(1, FAR, 0, far, h, fa_in)
    fa_in = swapped(fa1, 1)
    fb1 = edge(1, FAR, PART, far, h, fb_in)
    fb_in = swapped(fb1, 1)
    inner = functools.partial(inner_kernel, (NEAR,))
    (near2,) = stage(inner, [row], [], [x1, y1, near1, near_in, h, field])
    near_in = swapped(near2, 0)
    far, x2, y2 = stage(
        second_sweep_kernel, [wide, row, row], [], [fa1, fb1, x1, y1, near1, h, field], [scratch]
    )
    fa2 = edge(2, FAR, 0, far, h, fa_in)
    fa_in = swapped(fa2, 1)
    early = stage(
        early_kernel,
        group_structs(WIDE),
        [],
        [root, x2, y2, near2, near_in, h, y1, near1],
        [VMEM((2 * EY, NB, NB), BF)],
    )
    fb2 = edge(2, FAR, PART, far, h, fb_in)
    fb_in = swapped(fb2, 1)
    early = exchanged(early, 0)
    far, x = stage(
        third_sweep_kernel,
        [wide, row],
        [],
        [root, fa2, fb2, x2, y2, h, fa1, fb1, x1],
        [scratch, scratch],
    )
    late = stage(
        last_kernel,
        group_structs(WIDE),
        [],
        [root, far, h, fa_in, fb_in, x],
        [VMEM((2 * EY, NB, NB), BF)],
    )
    late = exchanged(late, 0)
    both = stage(second_kernel, group_structs(2 * THIN), [], [*early, *late])
    thin = [struct((THIN, NB), F32), struct((THIN, NB), BF)]
    own, sent = stage(third_kernel, thin, [], exchanged(both, 1))
    return stage(final_kernel, [struct((2, NB, NB), F32)], [], [own, across(sent)])[0]


def solution(mesh):
    return jax.shard_map(
        program,
        mesh=mesh,
        in_specs=(
            P("strip", None, "band"),
            P("strip", None, None, None),
            P("strip", None),
            P("band"),
        ),
        out_specs=P(("strip", "band"), None, None),
        check_vma=False,
    )
```
